32 devices in a mesh: ep: 2 (over z_hi), edp: 4 (over z_lo, core), etp: 4 (over y, x).
Axes of the slice: x: 2, y: 2, z: 4 (z_hi: 2, z_lo: 2; z = z_hi * 2 + z_lo), core: 2. Of those that a mesh axis runs over, the one named last changes fastest.
Arguments:
- rows_in: bfloat16 [2, 2, 96, 6144], P('ep', None, ('edp', 'etp')), may hold values from -6 to 6
- counts: int32 [2, 2, 4, 4], P('ep', None, 'edp', 'etp'), may hold values from 1 to 3, as said below
- gate_weight: bfloat16 [2, 6144, 8192], P('ep', 'edp', 'etp'), may hold values from -0.078125 to 0.078125
- up_weight: bfloat16 [2, 6144, 8192], P('ep', 'edp', 'etp'), may hold values from -0.078125 to 0.078125
- hid_grad: bfloat16 [2, 192, 8192], P('ep', 'edp', 'etp'), may hold values from -6 to 6
Outputs:
- act_factor: float32 [2, 4, 2048, 2048], P('ep', 'etp', 'edp')
- grad_factor: float32 [2, 4, 2048, 2048], P('ep', 'etp', 'edp')
The draws below stay inside these ranges and needn't reach their ends.
Inputs may be any that keep to these rules, and one draw needn't show every extreme that they name: `counts`: for every source, expert and edp index, the etp indices j and j + 2 hold 4 blocks together.
All inputs are finite; a program needn't handle non-finite values.
Results may differ from the reference program's by a relative error of at most 0.0042.
Values may be sent and summed in bfloat16 or wider, within the bound.
No kernel may reach another device: no remote copies, remote signals or barrier semaphores. Data moves between devices by JAX's collectives and lax.ppermute only.
A program may use at most 192 MiB of HBM per device.

```python
import jax
import jax.numpy as jnp
from jax import lax

D = 6144
HID = 8192
BROWS = 2
NBLK = 3
EXPERTS = 2
HALF = 6
ROWS_G = 48
SRC_ROWS = 96
ROWS = 192
BLK = 2048
TP_HALF = 2
LIVE = 128
N_EP = 2
N_EDP = 4
N_ETP = 4


def draw_counts(key, part):
    half_draw = jax.random.randint(key, (N_EP, EXPERTS, N_EDP, TP_HALF), 1, NBLK + 1, dtype=jnp.int32)
    half_draw = half_draw.at[0, 0, 0, 0].set(1)
    return jnp.concatenate([half_draw, NBLK + 1 - half_draw], axis=-1)


def shard_levels(key, dims, split, least, high):
    factor_of, own = 1.0, jax.random.fold_in(key, 6)
    for position, parts in split:
        heights = jnp.exp(jax.random.uniform(jax.random.fold_in(own, position), (parts,), jnp.float32, least / len(split), high / len(split)))
        factor_of = factor_of * jnp.repeat(heights, dims[position] // parts).reshape([-1 if axis == position else 1 for axis in range(len(dims))])
    return factor_of


def scatter_about(rng, shape, spread, most, cuts=(), kind=jnp.bfloat16):
    drawn = spread * jax.random.normal(rng, shape, jnp.float32)
    if cuts:
        drawn = drawn * shard_levels(rng, shape, cuts, -0.22, 0.18)
    return jnp.clip(drawn, -most, most).astype(kind)


def setup_inputs(seed: int = 0) -> dict:
    key_list = jax.random.split(jax.random.key(seed), 6)
    return {
        "rows_in": scatter_about(key_list[0], (N_EP, EXPERTS, SRC_ROWS, D), 1.0, 6.0, ((0, 2), (2, 16))),
        "counts": draw_counts(jax.random.fold_in(key_list[5], 71), 0),
        "gate_weight": scatter_about(key_list[2], (EXPERTS, D, HID), D ** -0.5, 0.078125, ((0, 2), (1, 4), (2, 4))),
        "up_weight": scatter_about(key_list[3], (EXPERTS, D, HID), D ** -0.5, 0.078125, ((0, 2), (1, 4), (2, 4))),
        "hid_grad": scatter_about(key_list[4], (EXPERTS, ROWS, HID), 1.0, 6.0, ((0, 2), (1, 4), (2, 4))),
    }


def reference(rows_in, counts, gate_weight, up_weight, hid_grad):
    act_list = []
    grad_list = []
    for expert in range(N_EP):
        rows_e = rows_in[:, expert].reshape(N_EP, N_EDP, N_ETP, HALF, D)
        rows_e = jnp.transpose(rows_e, (1, 2, 0, 3, 4)).reshape(N_EDP, ROWS_G, D)
        count_e = jnp.transpose(counts[:, expert], (1, 2, 0)).reshape(N_EDP, N_ETP * N_EP)
        grad_e = hid_grad[expert].reshape(N_EDP, ROWS_G, HID)
        gate_mat = gate_weight[expert]
        up_mat = up_weight[expert]

        def group_step(running, inputs):
            x_rows, block_counts, hid_grads = inputs
            gate_sum = jnp.dot(x_rows, gate_mat, preferred_element_type=jnp.float32)
            up_sum = jnp.dot(x_rows, up_mat, preferred_element_type=jnp.float32)
            slot_index = jnp.arange(HALF, dtype=jnp.int32)
            live_rows = (slot_index[None, :] < block_counts[:, None] * BROWS).reshape(ROWS_G)
            keep_rows = live_rows.astype(jnp.float32)[:, None]
            sigmoid_gate = jax.nn.sigmoid(gate_sum)
            hidden = (gate_sum * sigmoid_gate * up_sum * keep_rows).astype(jnp.bfloat16)
            gate_slope = sigmoid_gate * (1.0 + gate_sum * (1.0 - sigmoid_gate))
            gate_grad = (hid_grads.astype(jnp.float32) * up_sum * gate_slope * keep_rows).astype(jnp.bfloat16)
            hidden_blocks = hidden.astype(jnp.float32).reshape(ROWS_G, N_ETP, BLK)
            grad_blocks = gate_grad.astype(jnp.float32).reshape(ROWS_G, N_ETP, BLK)
            act_add = jnp.einsum("rjb,rjc->jbc", hidden_blocks, hidden_blocks, precision=lax.Precision.HIGHEST)
            grad_add = jnp.einsum("rjb,rjc->jbc", grad_blocks, grad_blocks, precision=lax.Precision.HIGHEST)
            return (running[0] + act_add, running[1] + grad_add), None

        zero_blocks = jnp.zeros((N_ETP, BLK, BLK), jnp.float32)
        (act_gram, grad_gram), unused = lax.scan(group_step, (zero_blocks, zero_blocks), (rows_e, count_e, grad_e))
        act_list.append(act_gram / LIVE)
        grad_list.append(grad_gram / LIVE)
    return jnp.stack(act_list), jnp.stack(grad_list)
```

```python
import functools
import math

import jax
import jax.numpy as jnp
from jax import lax
from jax.experimental import pallas as pl
from jax.experimental.pallas import tpu as pltpu
from jax.sharding import PartitionSpec as P

BROWS = 2
NBLK = 3
SLOT = (NBLK + 1) * BROWS
BF16 = jnp.bfloat16
F16 = jnp.float16
F32 = jnp.float32
ROW_MAX = 6.0
WEIGHT_MAX = 0.078125


def swap(value, axes, count, flip):
    return lax.ppermute(value, axes, [(i, i ^ flip) for i in range(count)])


def partial_kernel(half, high_ref, *refs):
    parts = refs[: 2 * half]
    wg = refs[2 * half : 2 * half + 2]
    wu = refs[2 * half + 2 : 2 * half + 4]
    keep_ref, send_ref, x_ref = refs[2 * half + 4 :]
    kept = keep_ref.shape[1]
    width = x_ref.shape[2]

    @pl.when(pl.program_id(0) == 0)
    def _():
        sources, chips, cores, slot = parts[0].shape[:4]
        for side in range(2):
            row = 0
            for core in range(cores):
                for chip in range(chips):
                    for col in range(half):
                        for source in range(sources):
                            block = parts[side * half + col][source, chip, core]
                            x_ref[side, row : row + slot, :] = block.astype(F32)
                            row += slot

    x0 = x_ref[0].astype(BF16)
    x1 = x_ref[1].astype(BF16)
    for index, w in enumerate((wg, wu)):
        total = jnp.dot(x0, w[0][0], preferred_element_type=F32)
        total += jnp.dot(x1, w[1][0], preferred_element_type=F32)
        keep_ref[index] = total[:kept]
        send_ref[index] = total[kept:]


def partial_sums(high, parts, gate_weight, up_weight):
    half = len(parts) // 2
    sources, chips, cores, slot, width = parts[0].shape
    rows = sources * chips * cores * slot * half
    kept = rows // 2
    columns = gate_weight.shape[1]
    block = min(columns, 512)
    weights = [w.reshape(2, width, columns) for w in (gate_weight, up_weight)]
    part_spec = pl.BlockSpec(parts[0].shape, lambda i, h: (0, 0, 0, 0, 0))
    near = pl.BlockSpec((1, width, block), lambda i, h: (h[0], 0, i))
    far = pl.BlockSpec((1, width, block), lambda i, h: (1 - h[0], 0, i))
    out = pl.BlockSpec((2, kept, block), lambda i, h: (0, 0, i))
    shape = jax.ShapeDtypeStruct((2, kept, columns), F32)
    return pl.pallas_call(
        functools.partial(partial_kernel, half),
        out_shape=(shape, shape),
        grid_spec=pltpu.PrefetchScalarGridSpec(
            num_scalar_prefetch=1,
            grid=(columns // block,),
            in_specs=[part_spec] * len(parts) + [near, far, near, far],
            out_specs=[out, out],
            scratch_shapes=[pltpu.VMEM((2, rows, width), F32)],
        ),
        cost_estimate=pl.CostEstimate(
            flops=4 * rows * 2 * width * columns,
            bytes_accessed=8 * width * columns,
            transcendentals=0,
        ),
        compiler_params=pltpu.CompilerParams(vmem_limit_bytes=32 << 20),
        name="partial_sums",
    )(high, *parts, weights[0], weights[0], weights[1], weights[1])


def gram_kernel(count, scale, owner_ref, *refs):
    parts = refs[:count]
    owned = refs[count : 2 * count]
    act_ref, grad_ref = refs[2 * count :]
    for index, out in enumerate((act_ref, grad_ref)):
        left = jnp.concatenate([p[index] for p in owned], axis=0)
        right = jnp.concatenate([p[index] for p in parts], axis=0)
        gram = lax.dot_general(left, right, (((0,), (0,)), ((), ())), preferred_element_type=F32)
        out[...] = gram * scale


def grams(owner, parts, owners, scale):
    columns = parts[0].shape[2]
    rows = parts[0].shape[1]
    own = columns // owners
    block = min(columns, 512)
    right = pl.BlockSpec((2, rows, block), lambda i, o: (0, 0, i))
    left = pl.BlockSpec((2, rows, own), lambda i, o: (0, 0, o[0]))
    out = pl.BlockSpec((own, block), lambda i, o: (0, i))
    if own % 128:
        left = pl.BlockSpec((2, rows, own), lambda i, o: (0, 0, 0))
        lefts = [lax.dynamic_slice_in_dim(p, owner[0] * own, own, 2) for p in parts]
    else:
        lefts = parts
    shape = jax.ShapeDtypeStruct((own, columns), F32)
    return pl.pallas_call(
        functools.partial(gram_kernel, len(parts), scale),
        out_shape=(shape, shape),
        grid_spec=pltpu.PrefetchScalarGridSpec(
            num_scalar_prefetch=1,
            grid=(columns // block,),
            in_specs=[right] * len(parts) + [left] * len(parts),
            out_specs=[out, out],
        ),
        compiler_params=pltpu.CompilerParams(vmem_limit_bytes=32 << 20),
        name="grams",
    )(owner, *parts, *lefts)


def body(rows_in, counts, gate_weight, up_weight, hid_grad):
    experts = lax.axis_size("ep")
    owners = lax.axis_size("edp")
    members = lax.axis_size("etp")
    half = members // 2
    chips = owners // 2
    half_rows = rows_in.shape[2]
    model_width = rows_in.shape[3]
    depth = model_width // owners // 2
    me_ep, me_edp, me_etp = (lax.axis_index(name) for name in ("ep", "edp", "etp"))
    chip, core = me_edp // 2, me_edp % 2
    high, col = me_etp // half, me_etp % half

    own_blocks = counts[0, :, 0, 0]
    low_blocks = jnp.where(high == 1, NBLK + 1 - own_blocks, own_blocks)
    low_here = lax.dynamic_index_in_dim(low_blocks, me_ep, 0, keepdims=True)
    by_source = [low_here]
    for flip in range(1, experts):
        away = lax.dynamic_index_in_dim(low_blocks, me_ep ^ flip, 0, keepdims=True)
        by_source.append(swap(away, "ep", experts, flip))
    source_counts = jnp.concatenate(by_source)
    pair_counts = [source_counts]
    for flip in range(1, half):
        pair_counts.append(swap(source_counts, "etp", members, flip))
    pair_counts = jnp.stack(pair_counts)

    live = own_blocks * BROWS
    offset = jnp.where(high == 1, SLOT - live, 0)
    source_row = jnp.arange(SLOT, dtype=jnp.int32)[None, :] - offset[:, None]
    valid = (source_row >= 0) & (source_row < live[:, None])
    pick = (source_row[:, :, None] == jnp.arange(half_rows, dtype=jnp.int32)) & valid[:, :, None]
    placed = jnp.einsum(
        "ekl,eld->ekd", pick.astype(BF16), rows_in[0], preferred_element_type=F32
    ).astype(BF16)
    pieces = placed.reshape(experts, SLOT, owners, 2, depth).transpose(3, 0, 2, 1, 4)
    mine = lax.dynamic_index_in_dim(pieces, high, 0, keepdims=False)
    theirs = lax.dynamic_index_in_dim(pieces, 1 - high, 0, keepdims=False)
    packed = mine + swap(theirs, "etp", members, half)

    by_core = packed.reshape(experts * chips, 2, SLOT, depth)
    stay = lax.dynamic_index_in_dim(by_core, core, 1, keepdims=False)
    leave = lax.dynamic_index_in_dim(by_core, 1 - core, 1, keepdims=False)
    paired = jnp.stack([stay, swap(leave, "edp", owners, 1)], axis=1)
    place = me_ep * chips + chip
    arrived = [lax.dynamic_index_in_dim(paired, place, 0, keepdims=False)]
    count = experts * owners
    for flip in range(1, experts * chips):
        piece = lax.dynamic_index_in_dim(paired, place ^ flip, 0, keepdims=False)
        arrived.append(swap(piece, ("ep", "edp"), count, flip * 2))
    slice_rows = jnp.stack(arrived).reshape(experts, chips, 2, SLOT, depth)
    parts = [slice_rows] + [swap(slice_rows, "etp", members, f) for f in range(1, members)]

    keep, send = partial_sums(high.reshape(1), parts, gate_weight[0], up_weight[0])
    group = keep.shape[1] // chips
    bound = model_width * ROW_MAX * WEIGHT_MAX
    scale = 2.0 ** math.floor(math.log2(float(jnp.finfo(F16).max) / bound))
    chip_sums = keep + swap((send * scale).astype(F16), "edp", owners, 1).astype(F32) / scale
    sums = chip_sums[:, :group]
    for flip in range(1, chips):
        away = chip_sums[:, flip * group : (flip + 1) * group]
        came = swap((away * scale).astype(F16), "edp", owners, 2 * flip)
        sums = sums + came.astype(F32) / scale

    pair_col = col ^ jnp.arange(half, dtype=jnp.int32)
    pair_source = me_ep ^ jnp.arange(experts, dtype=jnp.int32)
    slot = jnp.arange(SLOT, dtype=jnp.int32)[None, None, :]
    low_live = pair_counts[:, :, None] * BROWS
    low_row = (pair_col[:, None] * experts + pair_source[None, :])[:, :, None] * half_rows
    high_row = low_row + half * experts * half_rows
    row = jnp.where(slot < low_live, low_row + slot, high_row + slot - low_live).reshape(-1)
    group_rows = hid_grad.shape[1]
    choose = (row[:, None] == jnp.arange(group_rows, dtype=jnp.int32)).astype(BF16)
    hid_grads = jnp.dot(choose, hid_grad[0], preferred_element_type=F32)

    gate, up = sums[0], sums[1]
    sigmoid_gate = jax.nn.sigmoid(gate)
    hidden = (gate * sigmoid_gate * up).astype(BF16)
    gate_slope = sigmoid_gate * (1.0 + gate * (1.0 - sigmoid_gate))
    gate_grad = (hid_grads * up * gate_slope).astype(BF16)
    local = jnp.stack([hidden, gate_grad])

    gathered = [local] + [swap(local, "edp", owners, 2 * f) for f in range(1, chips)]
    gathered += [swap(part, "edp", owners, 1) for part in gathered]
    live_total = owners * experts * half * SLOT
    act, grad = grams(me_edp.reshape(1), gathered, owners, 1.0 / live_total)
    return act[None, None], grad[None, None]


def solution(mesh):
    in_specs = (
        P("ep", None, ("edp", "etp"), None),
        P("ep", None, "edp", "etp"),
        P("ep", "edp", "etp"),
        P("ep", "edp", "etp"),
        P("ep", "edp", "etp"),
    )
    out_specs = (P("ep", "etp", "edp", None), P("ep", "etp", "edp", None))
    return jax.shard_map(body, mesh=mesh, in_specs=in_specs, out_specs=out_specs, check_vma=False)
```

```python
import functools
import math

import jax
import jax.numpy as jnp
from jax import lax
from jax.experimental import pallas as pl
from jax.experimental.pallas import tpu as pltpu
from jax.sharding import PartitionSpec as P

BROWS = 2
NBLK = 3
SLOT = (NBLK + 1) * BROWS
LANES = 128
BF16 = jnp.bfloat16
F16 = jnp.float16
F32 = jnp.float32
ROW_MAX = 6.0
WEIGHT_MAX = 0.078125
PIECES = 4
GRAM_BLOCK = 512

VMEM = pl.BlockSpec(memory_space=pltpu.VMEM)


def limit(mib):
    return pltpu.CompilerParams(vmem_limit_bytes=mib << 20)


def swap(value, axes, count, flip):
    return lax.ppermute(value, axes, [(i, i ^ flip) for i in range(count)])


def after(first, *values):
    return lax.optimization_barrier((first, *values))[1:]


def hbm(value):
    return pltpu.with_memory_space_constraint(value, pltpu.HBM)


def weight_copies(src, dst, sems):
    step = src.shape[0] // PIECES
    spans = [pl.ds(piece * step, step) for piece in range(PIECES)]
    return [
        pltpu.make_async_copy(src.at[span], dst.at[span], sems.at[piece])
        for piece, span in enumerate(spans)
    ]


def place_kernel(counts_hbm, rows_hbm, *refs):
    stay_ref, leave_ref, counts_ref, rows_ref, wide_ref, count_sem, row_sem = refs
    _, slots, experts, _ = rows_ref.shape
    chips = stay_ref.shape[0] // experts
    depth = stay_ref.shape[2] - LANES
    high = lax.axis_index("etp") // (lax.axis_size("etp") // 2)
    core = lax.axis_index("edp") % 2
    here = lax.axis_index("ep") * chips + lax.axis_index("edp") // 2
    count_copy = pltpu.make_async_copy(counts_hbm, counts_ref, count_sem)
    row_copy = pltpu.make_async_copy(rows_hbm, rows_ref, row_sem)
    count_copy.start()
    row_copy.start()
    count_copy.wait()
    row_copy.wait()
    row = lax.broadcasted_iota(jnp.int32, wide_ref.shape, 0)
    for expert in range(experts):
        live = counts_ref[expert] * BROWS
        offset = high * (SLOT - live)
        wide_ref[slots:, :] = jnp.zeros_like(wide_ref[slots:, :])
        for slot in range(slots):
            wide_ref[slot, :] = rows_ref[0, slot, expert, :].astype(F32)
        moved = pltpu.roll(wide_ref[...], offset, 0)
        kept = (row >= offset) & (row < offset + live)
        wide_ref[...] = jnp.where(kept, moved, 0.0)
        low = jnp.where(kept[:, :LANES] & (high == 0), 1.0, 0.0).astype(BF16)
        for chip in range(chips):
            for side, out in enumerate((stay_ref, leave_ref)):
                start = pl.multiple_of((chip * 2 + (core ^ side)) * depth, LANES)
                spot = (expert * chips + chip) ^ here
                out[spot, :, :depth] = wide_ref[:, pl.ds(start, depth)].astype(BF16)
                out[spot, :, depth:] = low


def place(counts, rows, owners):
    _, _, experts, width = rows.shape
    shape = jax.ShapeDtypeStruct((experts * owners // 2, SLOT, width // owners + LANES), BF16)
    return pl.pallas_call(
        place_kernel,
        out_shape=(shape, shape),
        in_specs=[pl.BlockSpec(memory_space=pltpu.HBM)] * 2,
        out_specs=[VMEM, VMEM],
        scratch_shapes=[
            pltpu.SMEM(counts.shape, jnp.int32),
            pltpu.VMEM(rows.shape, BF16),
            pltpu.VMEM((SLOT, width), F32),
            pltpu.SemaphoreType.DMA,
            pltpu.SemaphoreType.DMA,
        ],
        compiler_params=limit(4),
        name="place",
    )(hbm(counts), hbm(rows))


def load_kernel(src, dst, sems):
    copies = weight_copies(src, dst, sems)
    for copy in copies:
        copy.start()
    for copy in copies:
        copy.wait()


def load_weight(weight):
    return pl.pallas_call(
        load_kernel,
        out_shape=pltpu.VMEM(weight.shape, weight.dtype),
        in_specs=[pl.BlockSpec(memory_space=pltpu.HBM)],
        out_specs=VMEM,
        scratch_shapes=[pltpu.SemaphoreType.DMA((PIECES,))],
        compiler_params=limit(4),
        name="load_weight",
    )(hbm(weight))


def gather_rows(part_ref, wide_ref, depth):
    chips, cores, slot, _ = part_ref.shape
    here = lax.axis_index("edp") // 2
    for core in range(cores):
        for chip in range(chips):
            start = pl.multiple_of((core * chips + (here ^ chip)) * slot, slot)
            wide_ref[pl.ds(start, slot), :] = part_ref[chip, core, :, :depth].astype(F32)
    return wide_ref[...].astype(BF16)


def first_kernel(part_ref, wg_ref, up_hbm, keep_ref, send_ref, wu_ref, wide_ref, sems):
    depth, columns = wg_ref.shape
    width = columns // PIECES
    spans = [pl.ds(piece * width, width) for piece in range(PIECES)]
    copies = [
        pltpu.make_async_copy(up_hbm.at[:, span], wu_ref.at[:, span], sems.at[piece])
        for piece, span in enumerate(spans)
    ]
    for copy in copies:
        copy.start()
    x = gather_rows(part_ref, wide_ref, depth)
    kept = keep_ref.shape[1]
    total = jnp.dot(x, wg_ref[...], preferred_element_type=F32)
    keep_ref[0] = total[:kept]
    send_ref[0] = total[kept:]
    for span, copy in zip(spans, copies):
        copy.wait()
        total = jnp.dot(x, wu_ref[:, span], preferred_element_type=F32)
        keep_ref[1, :, span] = total[:kept]
        send_ref[1, :, span] = total[kept:]


def first_sums(part, gate_weight, up_weight):
    chips, cores, slot, _ = part.shape
    depth, columns = gate_weight.shape
    rows = chips * cores * slot
    shape = jax.ShapeDtypeStruct((2, rows // 2, columns), F32)
    return pl.pallas_call(
        first_kernel,
        out_shape=(shape, shape, pltpu.VMEM(up_weight.shape, up_weight.dtype)),
        in_specs=[VMEM, VMEM, pl.BlockSpec(memory_space=pltpu.HBM)],
        out_specs=[VMEM] * 3,
        scratch_shapes=[pltpu.VMEM((rows, depth), F32), pltpu.SemaphoreType.DMA((PIECES,))],
        compiler_params=limit(8),
        name="first_sums",
    )(part, gate_weight, hbm(up_weight))


def partial_kernel(part_ref, wg_ref, wu_ref, keep_ref, send_ref, wide_ref):
    x = gather_rows(part_ref, wide_ref, wg_ref.shape[0])
    kept = keep_ref.shape[1]
    for index, w_ref in enumerate((wg_ref, wu_ref)):
        total = jnp.dot(x, w_ref[...], preferred_element_type=F32)
        keep_ref[index] = total[:kept]
        send_ref[index] = total[kept:]


def partial_sums(part, gate_weight, up_weight):
    chips, cores, slot, _ = part.shape
    depth, columns = gate_weight.shape
    rows = chips * cores * slot
    shape = jax.ShapeDtypeStruct((2, rows // 2, columns), F32)
    return pl.pallas_call(
        partial_kernel,
        out_shape=(shape, shape),
        in_specs=[VMEM] * 3,
        out_specs=[VMEM, VMEM],
        scratch_shapes=[pltpu.VMEM((rows, depth), F32)],
        compiler_params=limit(8),
        name="partial_sums",
    )(part, gate_weight, up_weight)


def select_kernel(chips, order, half_rows, *refs):
    hids, parts, (out_ref, pick_ref) = refs[:chips], refs[chips:-2], refs[-2:]
    experts, half = lax.axis_size("ep"), lax.axis_size("etp") // 2
    me_ep, col, here = lax.axis_index("ep"), lax.axis_index("etp") % half, lax.axis_index("edp") // 2
    _, _, slot, width = parts[0].shape
    group_rows = hids[0].shape[0]
    slot_row = lax.broadcasted_iota(jnp.int32, (slot, LANES), 0)
    column = lax.broadcasted_iota(jnp.int32, (slot, group_rows), 1)
    for flip in range(chips):
        for index, part in enumerate(parts):
            low = part[flip, 0, :, width - LANES :].astype(F32)
            lows = jnp.sum(low, axis=0, keepdims=True).astype(jnp.int32)
            low_row = ((col ^ order[index][0]) * experts + (me_ep ^ order[index][1])) * half_rows
            high_row = low_row + half * experts * half_rows
            row = jnp.where(low > 0.5, low_row + slot_row, high_row + slot_row - lows)
            pick = jnp.where(row[:, :1] == column, 1.0, 0.0)
            pick_ref[index * slot : (index + 1) * slot, :] = pick
        rows = jnp.dot(pick_ref[...].astype(BF16), hids[flip][...], preferred_element_type=F32)
        start = pl.multiple_of((here ^ flip) * slot, slot)
        for index in range(len(parts)):
            out_ref[index, pl.ds(start, slot), :] = rows[index * slot : (index + 1) * slot]


def select(order, half_rows, hids, parts):
    chips, _, slot, _ = parts[0].shape
    group_rows, columns = hids[0].shape
    return pl.pallas_call(
        functools.partial(select_kernel, chips, order, half_rows),
        out_shape=jax.ShapeDtypeStruct((len(parts), chips * slot, columns), F32),
        in_specs=[VMEM] * (chips + len(parts)),
        out_specs=VMEM,
        scratch_shapes=[pltpu.VMEM((len(parts) * slot, group_rows), F32)],
        compiler_params=limit(8),
        name="select",
    )(*hids, *parts)


def activate_kernel(index, sums_ref, hid_ref, both_ref):
    gate, up = sums_ref[0], sums_ref[1]
    sigmoid_gate = jax.nn.sigmoid(gate)
    both_ref[0] = (gate * sigmoid_gate * up).astype(BF16)
    gate_slope = sigmoid_gate * (1.0 + gate * (1.0 - sigmoid_gate))
    both_ref[1] = (hid_ref[index] * up * gate_slope).astype(BF16)


def activate(index, sums, hid):
    return pl.pallas_call(
        functools.partial(activate_kernel, index),
        out_shape=jax.ShapeDtypeStruct(sums.shape, BF16),
        in_specs=[VMEM, VMEM],
        out_specs=VMEM,
        compiler_params=limit(8),
        name="activate",
    )(sums, hid)


def gram_kernel(count, own, scale, *refs):
    parts = refs[:count]
    act_hbm, grad_hbm, all_ref, left_ref, out_ref, sems = refs[count:]
    rows = parts[0].shape[1]
    steps, _, block = out_ref.shape[1:]
    for index, part in enumerate(parts):
        all_ref[:, index * rows : (index + 1) * rows, :] = part[...]
    copies = []
    for index, out_hbm in enumerate((act_hbm, grad_hbm)):
        start = lax.axis_index("edp") * own
        if own % LANES == 0:
            left = all_ref[index, :, pl.ds(pl.multiple_of(start, LANES), own)]
        else:
            column = lax.broadcasted_iota(jnp.int32, (all_ref.shape[2], own), 0)
            wanted = lax.broadcasted_iota(jnp.int32, (all_ref.shape[2], own), 1) + start
            pick = jnp.where(column == wanted, 1.0, 0.0).astype(BF16)
            left = jnp.dot(all_ref[index], pick, preferred_element_type=F32).astype(BF16)
        left_ref[index] = left.T
        for step in range(steps):
            span = pl.ds(step * block, block)
            right = all_ref[index, :, span]
            gram = jnp.dot(left_ref[index], right, preferred_element_type=F32)
            out_ref[index, step] = gram * scale
            copy = pltpu.make_async_copy(
                out_ref.at[index, step], out_hbm.at[:, span], sems.at[index, step]
            )
            copy.start()
            copies.append(copy)
    for copy in copies:
        copy.wait()


def grams(parts, owners, scale):
    _, rows, columns = parts[0].shape
    own = columns // owners
    block = min(columns, GRAM_BLOCK)
    total = rows * len(parts)
    shape = jax.ShapeDtypeStruct((own, columns), F32)
    return pl.pallas_call(
        functools.partial(gram_kernel, len(parts), own, scale),
        out_shape=(shape, shape),
        in_specs=[VMEM] * len(parts),
        out_specs=[pl.BlockSpec(memory_space=pltpu.HBM)] * 2,
        scratch_shapes=[
            pltpu.VMEM((2, total, columns), BF16),
            pltpu.VMEM((2, own, total), BF16),
            pltpu.VMEM((2, columns // block, own, block), F32),
            pltpu.SemaphoreType.DMA((2, columns // block)),
        ],
        compiler_params=limit(24),
        name="grams",
    )(*parts)


def body(rows_in, counts, gate_weight, up_weight, hid_grad):
    experts = lax.axis_size("ep")
    owners = lax.axis_size("edp")
    members = lax.axis_size("etp")
    half = members // 2
    chips = owners // 2
    half_rows = rows_in.shape[2]
    model_width = rows_in.shape[3]
    order = [(flip, source) for flip in range(half) for source in range(experts)]
    hids = [hid_grad[0]]
    hids += [swap(hid_grad[0], "edp", owners, 2 * flip) for flip in range(1, chips)]
    stay, leave = place(counts.reshape(experts), jnp.swapaxes(rows_in, 1, 2), owners)
    came = swap(leave, "edp", owners, 1)
    arrived = []
    for flip in range(experts * chips):
        piece = jnp.stack([stay[flip], came[flip]])
        if flip:
            piece = swap(piece, ("ep", "edp"), experts * owners, 2 * flip)
        arrived.append(piece)

    met = []
    for source in range(experts):
        mine = jnp.stack(arrived[source * chips : (source + 1) * chips])
        met.append((mine, swap(mine, "etp", members, half)))
        if source == 0:
            (gate_out,) = after(mine, gate_weight[0])
            wg = load_weight(gate_out)

    bound = model_width * ROW_MAX * WEIGHT_MAX
    scale = 2.0 ** math.floor(math.log2(float(jnp.finfo(F16).max) / bound))
    parts, pairs = [None] * len(order), []
    chip_totals, leaves = [], []
    for index, (flip, source) in enumerate(order):
        if flip == 0:
            mine, theirs = met[source]
            if leaves:
                theirs, leaves[-1] = lax.optimization_barrier((theirs, leaves[-1]))
            pairs.append(mine + theirs)
            parts[index] = pairs[source]
            for other in range(1, half):
                moved = swap(pairs[source], "etp", members, other)
                parts[order.index((other, source))] = moved
        if index == 0:
            keep, send, wu = first_sums(parts[index], wg, up_weight[0])
        else:
            keep, send = partial_sums(parts[index], wg, wu)
        back = swap((send * scale).astype(F16), "edp", owners, 1)
        chip_totals.append(keep + back.astype(F32) / scale)
        leaves.append((chip_totals[index] * scale).astype(F16))
    hid = select(tuple(order), half_rows, hids, parts)
    local, across = [], []
    for index in range(len(order)):
        sums = chip_totals[index]
        for other in range(1, chips):
            there = swap(leaves[index], "edp", owners, 2 * other)
            sums = sums + there.astype(F32) / scale
        both = activate(index, sums, hid)
        local.append(both)
        across.append(swap(both, "edp", owners, 1))
    live_total = owners * experts * half * SLOT
    act, grad = grams(local + across, owners, 1.0 / live_total)
    return act[None, None], grad[None, None]


def solution(mesh):
    in_specs = (
        P("ep", None, ("edp", "etp"), None),
        P("ep", None, "edp", "etp"),
        P("ep", "edp", "etp"),
        P("ep", "edp", "etp"),
        P("ep", "edp", "etp"),
    )
    out_specs = (P("ep", "etp", "edp", None), P("ep", "etp", "edp", None))

    return jax.shard_map(body, mesh=mesh, in_specs=in_specs, out_specs=out_specs, check_vma=False)
```

```python
import functools
import math

import jax
import jax.numpy as jnp
from jax import lax
from jax.experimental import pallas as pl
from jax.experimental.pallas import tpu as pltpu
from jax.sharding import PartitionSpec as P

BROWS = 2
NBLK = 3
SLOT = (NBLK + 1) * BROWS
LANES = 128
BF16 = jnp.bfloat16
F16 = jnp.float16
F32 = jnp.float32
ROW_MAX = 6.0
WEIGHT_MAX = 0.078125
PIECES = 4
GRAM_BLOCK = 512
LAST_CUTS = 2

VMEM = pl.BlockSpec(memory_space=pltpu.VMEM)


def limit(mib):
    return pltpu.CompilerParams(vmem_limit_bytes=mib << 20)


def swap(value, axes, count, flip):
    return lax.ppermute(value, axes, [(i, i ^ flip) for i in range(count)])


def after(first, *values):
    return lax.optimization_barrier((first, *values))[1:]


def hbm(value):
    return pltpu.with_memory_space_constraint(value, pltpu.HBM)


def weight_copies(src, dst, sems):
    step = src.shape[0] // PIECES
    spans = [pl.ds(piece * step, step) for piece in range(PIECES)]
    return [
        pltpu.make_async_copy(src.at[span], dst.at[span], sems.at[piece])
        for piece, span in enumerate(spans)
    ]


def place_kernel(counts_hbm, rows_hbm, *refs):
    stay_ref, leave_ref, counts_ref, rows_ref, wide_ref, count_sem, row_sem = refs
    _, slots, experts, _ = rows_ref.shape
    chips = stay_ref.shape[0] // experts
    depth = stay_ref.shape[2] - LANES
    high = lax.axis_index("etp") // (lax.axis_size("etp") // 2)
    core = lax.axis_index("edp") % 2
    here = lax.axis_index("ep") * chips + lax.axis_index("edp") // 2
    count_copy = pltpu.make_async_copy(counts_hbm, counts_ref, count_sem)
    row_copy = pltpu.make_async_copy(rows_hbm, rows_ref, row_sem)
    count_copy.start()
    row_copy.start()
    count_copy.wait()
    row_copy.wait()
    row = lax.broadcasted_iota(jnp.int32, wide_ref.shape, 0)
    for expert in range(experts):
        live = counts_ref[expert] * BROWS
        offset = high * (SLOT - live)
        wide_ref[slots:, :] = jnp.zeros_like(wide_ref[slots:, :])
        for slot in range(slots):
            wide_ref[slot, :] = rows_ref[0, slot, expert, :].astype(F32)
        moved = pltpu.roll(wide_ref[...], offset, 0)
        kept = (row >= offset) & (row < offset + live)
        wide_ref[...] = jnp.where(kept, moved, 0.0)
        low = jnp.where(kept[:, :LANES] & (high == 0), 1.0, 0.0).astype(BF16)
        for chip in range(chips):
            for side, out in enumerate((stay_ref, leave_ref)):
                start = pl.multiple_of((chip * 2 + (core ^ side)) * depth, LANES)
                spot = (expert * chips + chip) ^ here
                out[spot, :, :depth] = wide_ref[:, pl.ds(start, depth)].astype(BF16)
                out[spot, :, depth:] = low


def place(counts, rows, owners):
    _, _, experts, width = rows.shape
    shape = jax.ShapeDtypeStruct((experts * owners // 2, SLOT, width // owners + LANES), BF16)
    return pl.pallas_call(
        place_kernel,
        out_shape=(shape, shape),
        in_specs=[pl.BlockSpec(memory_space=pltpu.HBM)] * 2,
        out_specs=[VMEM, VMEM],
        scratch_shapes=[
            pltpu.SMEM(counts.shape, jnp.int32),
            pltpu.VMEM(rows.shape, BF16),
            pltpu.VMEM((SLOT, width), F32),
            pltpu.SemaphoreType.DMA,
            pltpu.SemaphoreType.DMA,
        ],
        compiler_params=limit(4),
        name="place",
    )(hbm(counts), hbm(rows))


def load_kernel(gate_hbm, up_hbm, gate_ref, early_ref, sems, early_sem):
    copies = weight_copies(gate_hbm, gate_ref, sems)
    span = pl.ds(0, early_ref.shape[1])
    copies.append(pltpu.make_async_copy(up_hbm.at[:, span], early_ref, early_sem))
    for copy in copies:
        copy.start()
    for copy in copies:
        copy.wait()


def load_weights(gate_weight, up_weight):
    depth, columns = up_weight.shape
    return pl.pallas_call(
        load_kernel,
        out_shape=(
            pltpu.VMEM(gate_weight.shape, BF16),
            pltpu.VMEM((depth, columns // PIECES), BF16),
        ),
        in_specs=[pl.BlockSpec(memory_space=pltpu.HBM)] * 2,
        out_specs=[VMEM] * 2,
        scratch_shapes=[pltpu.SemaphoreType.DMA((PIECES,)), pltpu.SemaphoreType.DMA],
        compiler_params=limit(4),
        name="load_weights",
    )(hbm(gate_weight), hbm(up_weight))


def gather_rows(part_ref, wide_ref, depth):
    chips, cores, slot, _ = part_ref.shape
    here = lax.axis_index("edp") // 2
    for core in range(cores):
        for chip in range(chips):
            start = pl.multiple_of((core * chips + (here ^ chip)) * slot, slot)
            wide_ref[pl.ds(start, slot), :] = part_ref[chip, core, :, :depth].astype(F32)
    return wide_ref[...].astype(BF16)


def first_kernel(part_ref, wg_ref, early_ref, up_hbm, keep_ref, send_ref, late_ref, wide_ref, sems):
    depth, early = early_ref.shape
    copies = []
    for piece in range(PIECES - 1):
        src = up_hbm.at[:, pl.ds((piece + 1) * early, early)]
        dst = late_ref.at[:, pl.ds(piece * early, early)]
        copies.append(pltpu.make_async_copy(src, dst, sems.at[piece]))
    for copy in copies:
        copy.start()
    x = gather_rows(part_ref, wide_ref, depth)
    kept = keep_ref.shape[1]
    total = jnp.dot(x, wg_ref[...], preferred_element_type=F32)
    keep_ref[0] = total[:kept]
    send_ref[0] = total[kept:]
    for piece in range(PIECES):
        if piece:
            copies[piece - 1].wait()
            weight = late_ref[:, (piece - 1) * early : piece * early]
        else:
            weight = early_ref[...]
        total = jnp.dot(x, weight, preferred_element_type=F32)
        span = pl.ds(piece * early, early)
        keep_ref[1, :, span] = total[:kept]
        send_ref[1, :, span] = total[kept:]


def first_sums(part, gate_weight, early, up_weight):
    chips, cores, slot, _ = part.shape
    depth, columns = gate_weight.shape
    rows = chips * cores * slot
    shape = jax.ShapeDtypeStruct((2, rows // 2, columns), F32)
    return pl.pallas_call(
        first_kernel,
        out_shape=(shape, shape, pltpu.VMEM((depth, columns - early.shape[1]), BF16)),
        in_specs=[VMEM, VMEM, VMEM, pl.BlockSpec(memory_space=pltpu.HBM)],
        out_specs=[VMEM] * 3,
        scratch_shapes=[pltpu.VMEM((rows, depth), F32), pltpu.SemaphoreType.DMA((PIECES - 1,))],
        compiler_params=limit(8),
        name="first_sums",
    )(part, gate_weight, early, hbm(up_weight))


def partial_kernel(first, part_ref, wg_ref, early_ref, late_ref, keep_ref, send_ref, wide_ref):
    x = gather_rows(part_ref, wide_ref, wg_ref.shape[0])
    _, kept, width = keep_ref.shape
    early, last = early_ref.shape[1], first + width
    jobs = [(0, first, wg_ref, first, last)]
    if first < early:
        jobs.append((1, first, early_ref, first, min(early, last)))
    if last > early:
        jobs.append((1, max(first, early), late_ref, max(first, early) - early, last - early))
    for index, column, w_ref, begin, end in jobs:
        total = jnp.dot(x, w_ref[:, begin:end], preferred_element_type=F32)
        span = pl.ds(column - first, end - begin)
        keep_ref[index, :, span] = total[:kept]
        send_ref[index, :, span] = total[kept:]


def partial_sums(part, gate_weight, early, late, first, width):
    chips, cores, slot, _ = part.shape
    depth = gate_weight.shape[0]
    rows = chips * cores * slot
    shape = jax.ShapeDtypeStruct((2, rows // 2, width), F32)
    return pl.pallas_call(
        functools.partial(partial_kernel, first),
        out_shape=(shape, shape),
        in_specs=[VMEM] * 4,
        out_specs=[VMEM, VMEM],
        scratch_shapes=[pltpu.VMEM((rows, depth), F32)],
        cost_estimate=pl.CostEstimate(
            flops=4 * rows * depth * width, bytes_accessed=0, transcendentals=0
        ),
        compiler_params=limit(8),
        name="partial_sums",
    )(part, gate_weight, early, late)


def select_kernel(chips, order, half_rows, *refs):
    hids, parts, (out_ref, pick_ref) = refs[:chips], refs[chips:-2], refs[-2:]
    experts, half = lax.axis_size("ep"), lax.axis_size("etp") // 2
    me_ep, col, here = lax.axis_index("ep"), lax.axis_index("etp") % half, lax.axis_index("edp") // 2
    _, _, slot, width = parts[0].shape
    group_rows = hids[0].shape[0]
    slot_row = lax.broadcasted_iota(jnp.int32, (slot, LANES), 0)
    column = lax.broadcasted_iota(jnp.int32, (slot, group_rows), 1)
    for flip in range(chips):
        for index, part in enumerate(parts):
            low = part[flip, 0, :, width - LANES :].astype(F32)
            lows = jnp.sum(low, axis=0, keepdims=True).astype(jnp.int32)
            low_row = ((col ^ order[index][0]) * experts + (me_ep ^ order[index][1])) * half_rows
            high_row = low_row + half * experts * half_rows
            row = jnp.where(low > 0.5, low_row + slot_row, high_row + slot_row - lows)
            pick = jnp.where(row[:, :1] == column, 1.0, 0.0)
            pick_ref[index * slot : (index + 1) * slot, :] = pick
        rows = jnp.dot(pick_ref[...].astype(BF16), hids[flip][...], preferred_element_type=F32)
        start = pl.multiple_of((here ^ flip) * slot, slot)
        for index in range(len(parts)):
            out_ref[index, pl.ds(start, slot), :] = rows[index * slot : (index + 1) * slot]


def select(order, half_rows, hids, parts):
    chips, _, slot, _ = parts[0].shape
    group_rows, columns = hids[0].shape
    return pl.pallas_call(
        functools.partial(select_kernel, chips, order, half_rows),
        out_shape=jax.ShapeDtypeStruct((len(parts), chips * slot, columns), F32),
        in_specs=[VMEM] * (chips + len(parts)),
        out_specs=VMEM,
        scratch_shapes=[pltpu.VMEM((len(parts) * slot, group_rows), F32)],
        compiler_params=limit(8),
        name="select",
    )(*hids, *parts)


def activate_kernel(index, first, sums_ref, hid_ref, both_ref):
    gate, up = sums_ref[0], sums_ref[1]
    sigmoid_gate = jax.nn.sigmoid(gate)
    both_ref[0] = (gate * sigmoid_gate * up).astype(BF16)
    gate_slope = sigmoid_gate * (1.0 + gate * (1.0 - sigmoid_gate))
    both_ref[1] = (hid_ref[index, :, first : first + up.shape[1]] * up * gate_slope).astype(BF16)


def activate(index, first, sums, hid):
    return pl.pallas_call(
        functools.partial(activate_kernel, index, first),
        out_shape=jax.ShapeDtypeStruct(sums.shape, BF16),
        in_specs=[VMEM, VMEM],
        out_specs=VMEM,
        compiler_params=limit(8),
        name="activate",
    )(sums, hid)


def gram_kernel(spots, own, scale, *refs):
    count = len(spots)
    parts = refs[:count]
    act_hbm, grad_hbm, all_ref, left_ref, out_ref, sems = refs[count:]
    steps, _, block = out_ref.shape[1:]
    for (row, first), part in zip(spots, parts):
        _, rows, width = part.shape
        all_ref[:, row : row + rows, first : first + width] = part[...]
    copies = []
    for index, out_hbm in enumerate((act_hbm, grad_hbm)):
        start = lax.axis_index("edp") * own
        if own % LANES == 0:
            left = all_ref[index, :, pl.ds(pl.multiple_of(start, LANES), own)]
        else:
            column = lax.broadcasted_iota(jnp.int32, (all_ref.shape[2], own), 0)
            wanted = lax.broadcasted_iota(jnp.int32, (all_ref.shape[2], own), 1) + start
            pick = jnp.where(column == wanted, 1.0, 0.0).astype(BF16)
            left = jnp.dot(all_ref[index], pick, preferred_element_type=F32).astype(BF16)
        left_ref[index] = left.T
        for step in range(steps):
            span = pl.ds(step * block, block)
            right = all_ref[index, :, span]
            gram = jnp.dot(left_ref[index], right, preferred_element_type=F32)
            out_ref[index, step] = gram * scale
            copy = pltpu.make_async_copy(
                out_ref.at[index, step], out_hbm.at[:, span], sems.at[index, step]
            )
            copy.start()
            copies.append(copy)
    for copy in copies:
        copy.wait()


def grams(parts, spots, columns, owners, scale):
    own = columns // owners
    block = min(columns, GRAM_BLOCK)
    total = max(row for row, _ in spots) + parts[0].shape[1]
    shape = jax.ShapeDtypeStruct((own, columns), F32)
    return pl.pallas_call(
        functools.partial(gram_kernel, tuple(spots), own, scale),
        out_shape=(shape, shape),
        in_specs=[VMEM] * len(parts),
        out_specs=[pl.BlockSpec(memory_space=pltpu.HBM)] * 2,
        scratch_shapes=[
            pltpu.VMEM((2, total, columns), BF16),
            pltpu.VMEM((2, own, total), BF16),
            pltpu.VMEM((2, columns // block, own, block), F32),
            pltpu.SemaphoreType.DMA((2, columns // block)),
        ],
        compiler_params=limit(24),
        name="grams",
    )(*parts)


def body(rows_in, counts, gate_weight, up_weight, hid_grad):
    experts = lax.axis_size("ep")
    owners = lax.axis_size("edp")
    members = lax.axis_size("etp")
    half = members // 2
    chips = owners // 2
    half_rows = rows_in.shape[2]
    model_width = rows_in.shape[3]
    order = [(flip, source) for flip in range(half) for source in range(experts)]
    hids = [hid_grad[0]]
    hids += [swap(hid_grad[0], "edp", owners, 2 * flip) for flip in range(1, chips)]
    stay, leave = place(counts.reshape(experts), jnp.swapaxes(rows_in, 1, 2), owners)
    came = swap(leave, "edp", owners, 1)
    arrived = []
    for flip in range(experts * chips):
        piece = jnp.stack([stay[flip], came[flip]])
        if flip:
            piece = swap(piece, ("ep", "edp"), experts * owners, 2 * flip)
        arrived.append(piece)

    met = []
    for source in range(experts):
        mine = jnp.stack(arrived[source * chips : (source + 1) * chips])
        met.append((mine, swap(mine, "etp", members, half)))
        if source == 0:
            gate_out, up_out = after(mine, gate_weight[0], up_weight[0])
            wg, early = load_weights(gate_out, up_out)

    bound = model_width * ROW_MAX * WEIGHT_MAX
    scale = 2.0 ** math.floor(math.log2(float(jnp.finfo(F16).max) / bound))
    columns = gate_weight.shape[2]
    cuts = [1] * (len(order) - 1) + [LAST_CUTS if columns % (LAST_CUTS * LANES) == 0 else 1]
    parts, pairs = [None] * len(order), []
    tags, chip_totals, leaves = [], [], []
    for index, (flip, source) in enumerate(order):
        if flip == 0:
            mine, theirs = met[source]
            if leaves:
                theirs, leaves[-1] = lax.optimization_barrier((theirs, leaves[-1]))
            pairs.append(mine + theirs)
            parts[index] = pairs[source]
            for other in range(1, half):
                moved = swap(pairs[source], "etp", members, other)
                parts[order.index((other, source))] = moved
        width = columns // cuts[index]
        for first in range(0, columns, width):
            tag = str(len(tags))
            tags.append((index, first))
            if index == 0:
                keep, send, late = first_sums(parts[index], wg, early, up_weight[0])
            else:
                keep, send = partial_sums(parts[index], wg, early, late, first, width)
            back = swap((send * scale).astype(F16), "edp", owners, 1)
            chip_totals.append(keep + back.astype(F32) / scale)
            leaves.append((chip_totals[-1] * scale).astype(F16))
    hid = select(tuple(order), half_rows, hids, parts)
    local, across, spots = [], [], []
    for tag, (index, first) in enumerate(tags):
        sums = chip_totals[tag]
        for other in range(1, chips):
            there = swap(leaves[tag], "edp", owners, 2 * other)
            sums = sums + there.astype(F32) / scale
        both = activate(index, first, sums, hid)
        local.append(both)
        spots.append((index * both.shape[1], first))
        across.append(swap(both, "edp", owners, 1))
    total = len(order) * local[0].shape[1]
    spots += [(total + row, first) for row, first in spots]
    live_total = owners * experts * half * SLOT
    act, grad = grams(local + across, spots, columns, owners, 1.0 / live_total)
    return act[None, None], grad[None, None]


def solution(mesh):
    in_specs = (
        P("ep", None, ("edp", "etp"), None),
        P("ep", None, "edp", "etp"),
        P("ep", "edp", "etp"),
        P("ep", "edp", "etp"),
        P("ep", "edp", "etp"),
    )
    out_specs = (P("ep", "etp", "edp", None), P("ep", "etp", "edp", None))

    return jax.shard_map(body, mesh=mesh, in_specs=in_specs, out_specs=out_specs, check_vma=False)
```

```python
import functools
import math

import jax
import jax.numpy as jnp
from jax import lax
from jax.experimental import pallas as pl
from jax.experimental.pallas import tpu as pltpu
from jax.sharding import PartitionSpec as P

BROWS = 2
NBLK = 3
SLOT = (NBLK + 1) * BROWS
LANES = 128
BF16 = jnp.bfloat16
F16 = jnp.float16
F32 = jnp.float32
ROW_MAX = 6.0
WEIGHT_MAX = 0.078125
PIECES = 4
GRAM_BLOCK = 512
CUTS = 2

VMEM = pl.BlockSpec(memory_space=pltpu.VMEM)


def limit(mib):
    return pltpu.CompilerParams(vmem_limit_bytes=mib << 20)


def swap(value, axes, count, flip):
    return lax.ppermute(value, axes, [(i, i ^ flip) for i in range(count)])


def after(first, *values):
    return lax.optimization_barrier((first, *values))[1:]


def hbm(value):
    return pltpu.with_memory_space_constraint(value, pltpu.HBM)


def weight_copies(src, dst, sems):
    step = src.shape[0] // PIECES
    spans = [pl.ds(piece * step, step) for piece in range(PIECES)]
    return [
        pltpu.make_async_copy(src.at[span], dst.at[span], sems.at[piece])
        for piece, span in enumerate(spans)
    ]


def place_kernel(counts_hbm, rows_hbm, *refs):
    stay_ref, leave_ref, counts_ref, rows_ref, wide_ref, count_sem, row_sem = refs
    _, slots, experts, _ = rows_ref.shape
    chips = stay_ref.shape[0] // experts
    depth = stay_ref.shape[2] - LANES
    high = lax.axis_index("etp") // (lax.axis_size("etp") // 2)
    core = lax.axis_index("edp") % 2
    here = lax.axis_index("ep") * chips + lax.axis_index("edp") // 2
    count_copy = pltpu.make_async_copy(counts_hbm, counts_ref, count_sem)
    row_copy = pltpu.make_async_copy(rows_hbm, rows_ref, row_sem)
    count_copy.start()
    row_copy.start()
    count_copy.wait()
    row_copy.wait()
    row = lax.broadcasted_iota(jnp.int32, wide_ref.shape, 0)
    for expert in range(experts):
        live = counts_ref[expert] * BROWS
        offset = high * (SLOT - live)
        wide_ref[slots:, :] = jnp.zeros_like(wide_ref[slots:, :])
        for slot in range(slots):
            wide_ref[slot, :] = rows_ref[0, slot, expert, :].astype(F32)
        moved = pltpu.roll(wide_ref[...], offset, 0)
        kept = (row >= offset) & (row < offset + live)
        wide_ref[...] = jnp.where(kept, moved, 0.0)
        low = jnp.where(kept[:, :LANES] & (high == 0), 1.0, 0.0).astype(BF16)
        for chip in range(chips):
            for side, out in enumerate((stay_ref, leave_ref)):
                start = pl.multiple_of((chip * 2 + (core ^ side)) * depth, LANES)
                spot = (expert * chips + chip) ^ here
                out[spot, :, :depth] = wide_ref[:, pl.ds(start, depth)].astype(BF16)
                out[spot, :, depth:] = low


def place(counts, rows, owners):
    _, _, experts, width = rows.shape
    shape = jax.ShapeDtypeStruct((experts * owners // 2, SLOT, width // owners + LANES), BF16)
    return pl.pallas_call(
        place_kernel,
        out_shape=(shape, shape),
        in_specs=[pl.BlockSpec(memory_space=pltpu.HBM)] * 2,
        out_specs=[VMEM, VMEM],
        scratch_shapes=[
            pltpu.SMEM(counts.shape, jnp.int32),
            pltpu.VMEM(rows.shape, BF16),
            pltpu.VMEM((SLOT, width), F32),
            pltpu.SemaphoreType.DMA,
            pltpu.SemaphoreType.DMA,
        ],
        compiler_params=limit(4),
        name="place",
    )(hbm(counts), hbm(rows))


def load_kernel(src, dst, sems):
    copies = weight_copies(src, dst, sems)
    for copy in copies:
        copy.start()
    for copy in copies:
        copy.wait()


def load_weight(weight):
    return pl.pallas_call(
        load_kernel,
        out_shape=pltpu.VMEM(weight.shape, weight.dtype),
        in_specs=[pl.BlockSpec(memory_space=pltpu.HBM)],
        out_specs=VMEM,
        scratch_shapes=[pltpu.SemaphoreType.DMA((PIECES,))],
        compiler_params=limit(4),
        name="load_weight",
    )(hbm(weight))


def partial_kernel(first, *refs):
    parts, (wg_ref, wu_ref, keep_ref, send_ref, wide_ref) = refs[:-5], refs[-5:]
    chips, cores, slot, _ = parts[0].shape
    depth = wg_ref.shape[0]
    here = lax.axis_index("edp") // 2
    for core in range(cores):
        for source, part in enumerate(parts):
            for chip in range(chips):
                block = (core * len(parts) + source) * chips + (here ^ chip)
                start = pl.multiple_of(block * slot, slot)
                wide_ref[pl.ds(start, slot), :] = part[chip, core, :, :depth].astype(F32)
    x = wide_ref[...].astype(BF16)
    _, kept, width = keep_ref.shape
    for index, w_ref in enumerate((wg_ref, wu_ref)):
        total = jnp.dot(x, w_ref[:, first : first + width], preferred_element_type=F32)
        keep_ref[index] = total[:kept]
        send_ref[index] = total[kept:]


def partial_sums(parts, gate_weight, up_weight, first, width):
    chips, cores, slot, _ = parts[0].shape
    depth = gate_weight.shape[0]
    rows = len(parts) * chips * cores * slot
    shape = jax.ShapeDtypeStruct((2, rows // 2, width), F32)
    return pl.pallas_call(
        functools.partial(partial_kernel, first),
        out_shape=(shape, shape),
        in_specs=[VMEM] * (len(parts) + 2),
        out_specs=[VMEM, VMEM],
        scratch_shapes=[pltpu.VMEM((rows, depth), F32)],
        cost_estimate=pl.CostEstimate(
            flops=4 * rows * depth * width, bytes_accessed=0, transcendentals=0
        ),
        compiler_params=limit(8),
        name="partial_sums",
    )(*parts, gate_weight, up_weight)


def select_kernel(chips, order, half_rows, *refs):
    hids, parts, (out_ref, pick_ref) = refs[:chips], refs[chips:-2], refs[-2:]
    experts, half = lax.axis_size("ep"), lax.axis_size("etp") // 2
    me_ep, col, here = lax.axis_index("ep"), lax.axis_index("etp") % half, lax.axis_index("edp") // 2
    _, _, slot, width = parts[0].shape
    group_rows = hids[0].shape[0]
    slot_row = lax.broadcasted_iota(jnp.int32, (slot, LANES), 0)
    column = lax.broadcasted_iota(jnp.int32, (slot, group_rows), 1)
    for flip in range(chips):
        for index, part in enumerate(parts):
            low = part[flip, 0, :, width - LANES :].astype(F32)
            lows = jnp.sum(low, axis=0, keepdims=True).astype(jnp.int32)
            low_row = ((col ^ order[index][0]) * experts + (me_ep ^ order[index][1])) * half_rows
            high_row = low_row + half * experts * half_rows
            row = jnp.where(low > 0.5, low_row + slot_row, high_row + slot_row - lows)
            pick = jnp.where(row[:, :1] == column, 1.0, 0.0)
            pick_ref[index * slot : (index + 1) * slot, :] = pick
        rows = jnp.dot(pick_ref[...].astype(BF16), hids[flip][...], preferred_element_type=F32)
        for index in range(len(parts)):
            block = index % experts * chips + (here ^ flip)
            start = pl.multiple_of(block * slot, slot)
            out_ref[index // experts, pl.ds(start, slot), :] = rows[index * slot : (index + 1) * slot]


def select(order, half_rows, groups, hids, parts):
    chips, _, slot, _ = parts[0].shape
    group_rows, columns = hids[0].shape
    return pl.pallas_call(
        functools.partial(select_kernel, chips, order, half_rows),
        out_shape=jax.ShapeDtypeStruct((groups, len(parts) // groups * chips * slot, columns), F32),
        in_specs=[VMEM] * (chips + len(parts)),
        out_specs=VMEM,
        scratch_shapes=[pltpu.VMEM((len(parts) * slot, group_rows), F32)],
        compiler_params=limit(8),
        name="select",
    )(*hids, *parts)


def activate_kernel(index, first, sums_ref, hid_ref, both_ref):
    gate, up = sums_ref[0], sums_ref[1]
    sigmoid_gate = jax.nn.sigmoid(gate)
    both_ref[0] = (gate * sigmoid_gate * up).astype(BF16)
    gate_slope = sigmoid_gate * (1.0 + gate * (1.0 - sigmoid_gate))
    both_ref[1] = (hid_ref[index, :, first : first + up.shape[1]] * up * gate_slope).astype(BF16)


def activate(index, first, sums, hid):
    return pl.pallas_call(
        functools.partial(activate_kernel, index, first),
        out_shape=jax.ShapeDtypeStruct(sums.shape, BF16),
        in_specs=[VMEM, VMEM],
        out_specs=VMEM,
        compiler_params=limit(8),
        name="activate",
    )(sums, hid)


def gram_kernel(spots, own, scale, *refs):
    count = len(spots)
    parts = refs[:count]
    act_hbm, grad_hbm, all_ref, left_ref, out_ref, sems = refs[count:]
    steps, _, block = out_ref.shape[1:]
    for (row, first), part in zip(spots, parts):
        _, rows, width = part.shape
        all_ref[:, row : row + rows, first : first + width] = part[...]
    copies = []
    for index, out_hbm in enumerate((act_hbm, grad_hbm)):
        start = lax.axis_index("edp") * own
        if own % LANES == 0:
            left = all_ref[index, :, pl.ds(pl.multiple_of(start, LANES), own)]
        else:
            column = lax.broadcasted_iota(jnp.int32, (all_ref.shape[2], own), 0)
            wanted = lax.broadcasted_iota(jnp.int32, (all_ref.shape[2], own), 1) + start
            pick = jnp.where(column == wanted, 1.0, 0.0).astype(BF16)
            left = jnp.dot(all_ref[index], pick, preferred_element_type=F32).astype(BF16)
        left_ref[index] = left.T
        for step in range(steps):
            span = pl.ds(step * block, block)
            right = all_ref[index, :, span]
            gram = jnp.dot(left_ref[index], right, preferred_element_type=F32)
            out_ref[index, step] = gram * scale
            copy = pltpu.make_async_copy(
                out_ref.at[index, step], out_hbm.at[:, span], sems.at[index, step]
            )
            copy.start()
            copies.append(copy)
    for copy in copies:
        copy.wait()


def grams(parts, spots, columns, owners, scale):
    own = columns // owners
    block = min(columns, GRAM_BLOCK)
    total = max(row for row, _ in spots) + parts[0].shape[1]
    shape = jax.ShapeDtypeStruct((own, columns), F32)
    return pl.pallas_call(
        functools.partial(gram_kernel, tuple(spots), own, scale),
        out_shape=(shape, shape),
        in_specs=[VMEM] * len(parts),
        out_specs=[pl.BlockSpec(memory_space=pltpu.HBM)] * 2,
        scratch_shapes=[
            pltpu.VMEM((2, total, columns), BF16),
            pltpu.VMEM((2, own, total), BF16),
            pltpu.VMEM((2, columns // block, own, block), F32),
            pltpu.SemaphoreType.DMA((2, columns // block)),
        ],
        compiler_params=limit(24),
        name="grams",
    )(*parts)


def body(rows_in, counts, gate_weight, up_weight, hid_grad):
    experts = lax.axis_size("ep")
    owners = lax.axis_size("edp")
    members = lax.axis_size("etp")
    half = members // 2
    chips = owners // 2
    half_rows = rows_in.shape[2]
    model_width = rows_in.shape[3]
    order = [(flip, source) for flip in range(half) for source in range(experts)]
    hids = [hid_grad[0]]
    hids += [swap(hid_grad[0], "edp", owners, 2 * flip) for flip in range(1, chips)]
    stay, leave = place(counts.reshape(experts), jnp.swapaxes(rows_in, 1, 2), owners)
    came = swap(leave, "edp", owners, 1)
    arrived = []
    for flip in range(experts * chips):
        piece = jnp.stack([stay[flip], came[flip]])
        if flip:
            piece = swap(piece, ("ep", "edp"), experts * owners, 2 * flip)
        arrived.append(piece)

    met = []
    for source in range(experts):
        mine = jnp.stack(arrived[source * chips : (source + 1) * chips])
        met.append((mine, swap(mine, "etp", members, half)))
        if source == 0:
            (gate_out,) = after(mine, gate_weight[0])
            wg = load_weight(gate_out)
        else:
            (up_out,) = after(mine, up_weight[0])
            if source == 1:
                wu = load_weight(up_out)

    bound = model_width * ROW_MAX * WEIGHT_MAX
    scale = 2.0 ** math.floor(math.log2(float(jnp.finfo(F16).max) / bound))
    columns = gate_weight.shape[2]
    width = columns // CUTS if columns % (CUTS * LANES) == 0 else columns
    pairs = []
    for mine, theirs in met:
        pairs.append(mine + theirs)
    parts = []
    for flip, source in order:
        part = pairs[source]
        if flip:
            part = swap(part, "etp", members, flip)
        parts.append(part)
    tags, chip_totals, leaves = [], [], []
    for flip in range(half):
        group = parts[flip * experts : (flip + 1) * experts]
        for first in range(0, columns, width):
            tag = str(len(tags))
            tags.append((flip, first))
            keep, send = partial_sums(group, wg, wu, first, width)
            back = swap((send * scale).astype(F16), "edp", owners, 1)
            chip_totals.append(keep + back.astype(F32) / scale)
            leaves.append((chip_totals[-1] * scale).astype(F16))
    hid = select(tuple(order), half_rows, half, hids, parts)
    local, across, spots = [], [], []
    for tag, (index, first) in enumerate(tags):
        sums = chip_totals[tag]
        for other in range(1, chips):
            there = swap(leaves[tag], "edp", owners, 2 * other)
            sums = sums + there.astype(F32) / scale
        both = activate(index, first, sums, hid)
        local.append(both)
        spots.append((index * both.shape[1], first))
        across.append(swap(both, "edp", owners, 1))
    total = half * local[0].shape[1]
    spots += [(total + row, first) for row, first in spots]
    live_total = owners * experts * half * SLOT
    act, grad = grams(local + across, spots, columns, owners, 1.0 / live_total)
    return act[None, None], grad[None, None]


def solution(mesh):
    in_specs = (
        P("ep", None, ("edp", "etp"), None),
        P("ep", None, "edp", "etp"),
        P("ep", "edp", "etp"),
        P("ep", "edp", "etp"),
        P("ep", "edp", "etp"),
    )
    out_specs = (P("ep", "etp", "edp", None), P("ep", "etp", "edp", None))

    return jax.shard_map(body, mesh=mesh, in_specs=in_specs, out_specs=out_specs, check_vma=False)
```
